32 devices in a mesh: dp: 8 (over z, y), mp: 4 (over x, core).
Axes of the slice: x: 2, y: 2, z: 4, core: 2. Of those that a mesh axis runs over, the one named last changes fastest.
Arguments:
- tokens: bfloat16 [24576, 768], P('dp'), may hold values from -6 to 6
- out_grad: bfloat16 [24576, 768], P('dp'), may hold values from -6 to 6
- pair_start: int32 [48, 12], P('dp'), may hold values from 0 to 471, as said below
- caption_len: int32 [48, 12], P('dp'), may hold values from 0 to 60, as said below
- region_len: int32 [48, 12], P('dp'), may hold values from 0 to 100, as said below
- w_query: bfloat16 [768, 768], P(None, 'mp'), may hold values from -0.21875 to 0.21875
- w_key: bfloat16 [768, 768], P(None, 'mp'), may hold values from -0.21875 to 0.21875
- w_value: bfloat16 [768, 768], P(None, 'mp'), may hold values from -0.21875 to 0.21875
- b_query: float32 [768], P('mp'), may hold values from -3 to 3
- b_value: float32 [768], P('mp'), may hold values from -3 to 3
- w_out: bfloat16 [768, 768], P('mp'), may hold values from -1.25 to 1.25
- b_out: float32 [768], replicated, may hold values from -2 to 2
- mixed_gain: float32 [768], replicated, may hold values from 0.5 to 1.5
- mixed_shift: float32 [768], replicated, may hold values from -2 to 2
- w_up: bfloat16 [768, 3072], P(None, 'mp'), may hold values from -0.21875 to 0.21875
- b_up: float32 [3072], P('mp'), may hold values from -3 to 3
- w_down: bfloat16 [3072, 768], P('mp'), may hold values from -0.109375 to 0.109375
- b_down: float32 [768], replicated, may hold values from -2 to 2
- final_gain: float32 [768], replicated, may hold values from 0.5 to 1.5
- final_shift: float32 [768], replicated, may hold values from -2 to 2
Outputs:
- layer_out: bfloat16 [24576, 768], P(('dp', 'mp'))
- tokens_grad: bfloat16 [24576, 768], P(('dp', 'mp'))
- w_query_grad: float32 [768, 768], P('dp', 'mp')
- w_key_grad: float32 [768, 768], P('dp', 'mp')
- w_value_grad: float32 [768, 768], P('dp', 'mp')
- b_query_grad: float32 [768], P(('mp', 'dp'))
- b_value_grad: float32 [768], P(('mp', 'dp'))
- w_out_grad: float32 [768, 768], P('mp', 'dp')
- b_out_grad: float32 [768], P('dp')
- mixed_gain_grad: float32 [768], P(('dp', 'mp'))
- mixed_shift_grad: float32 [768], P(('dp', 'mp'))
- w_up_grad: float32 [768, 3072], P('dp', 'mp')
- b_up_grad: float32 [3072], P(('mp', 'dp'))
- w_down_grad: float32 [3072, 768], P('mp', 'dp')
- b_down_grad: float32 [768], P('dp')
- final_gain_grad: float32 [768], P(('dp', 'mp'))
- final_shift_grad: float32 [768], P(('dp', 'mp'))
The draws below stay inside these ranges and needn't reach their ends.
Inputs may be any that keep to these rules, and one draw needn't show every extreme that they name: In each packed block the used slots come first; a used slot starts where the one before it ends (the first at 0), holds caption_len of 5 to 60 and region_len of 36 to 100, and all used pairs end by 512; unused slots have pair_start 0. `caption_len`: 0 marks an unused slot; some block holds a pair of 60 caption words. `region_len`: 0 marks an unused slot; some pair with 60 caption words has 100 regions.
All inputs are finite; a program needn't handle non-finite values.
Results may differ from the reference program's by a relative error of at most 0.03.
Values may be sent and summed in bfloat16 or wider, within the bound.
A program may use at most 256 MiB of HBM per device.

```python
import math
import jax
import jax.numpy as jnp
from jax import lax

D = 768
HEADS = 12
HD = 64
FF = 3072
BIN = 512
CAP_MIN = 5
CAP_MAX = 60
REG_MIN = 36
REG_MAX = 100
SLOTS = 12
TOKENS = 24576
BINS = 48
N_MP = 4


def pair_tables(key):
    streams = jax.random.split(jax.random.fold_in(key, 7), 3)
    spread = CAP_MAX - CAP_MIN
    base = jax.random.randint(streams[0], (BINS, SLOTS), 0, spread + 1)
    captions = CAP_MIN + base * base * base // max(spread * spread, 1)
    regions = jax.random.randint(streams[1], (BINS, SLOTS), REG_MIN, REG_MAX + 1)
    chosen = jax.random.randint(streams[2], (), 0, BINS)
    marked = (jnp.arange(BINS)[:, None] == chosen) & (jnp.arange(SLOTS)[None, :] == 0)
    captions = jnp.where(marked, CAP_MAX, captions)
    regions = jnp.where(marked, REG_MAX, regions)
    lengths = captions + regions
    finish = jnp.cumsum(lengths, axis=1)
    keeping = finish <= BIN
    starts = jnp.where(keeping, finish - lengths, 0)
    return (starts.astype(jnp.int32), jnp.where(keeping, captions, 0).astype(jnp.int32), jnp.where(keeping, regions, 0).astype(jnp.int32))


def draw_pair_start(key, part):
    return pair_tables(key)[0]


def draw_caption_len(key, part):
    return pair_tables(key)[1]


def draw_region_len(key, part):
    return pair_tables(key)[2]


def with_spikes(array, own_key, source, target, blocks, factor):
    def block_of(axis_at):
        return (jnp.arange(array.shape[axis_at]) // (array.shape[axis_at] // blocks)).reshape((-1,) + (1,) * (array.ndim - 1 - axis_at))

    first = jax.random.permutation(own_key, blocks)[block_of(target)]
    far = (block_of(target) + blocks // 2) % blocks
    return jnp.where((block_of(source) == first) | (block_of(source) == far), factor * array, array)


def shard_levels(rng, dims, shards, smallest, top_value):
    def one(position, blocks):
        steps = jax.random.uniform(jax.random.fold_in(jax.random.fold_in(rng, 6), position), (blocks,), jnp.float32, smallest / len(shards), top_value / len(shards))
        return jnp.repeat(jnp.exp(steps), dims[position] // blocks).reshape((-1,) + (1,) * (len(dims) - position - 1))

    factor_of = one(*shards[0])
    for cut in shards[1:]:
        factor_of = factor_of * one(*cut)
    return factor_of


def gaussian(stream_key, dims, width, most, cuts=(), kind=jnp.bfloat16):
    factor_of = shard_levels(stream_key, dims, cuts, -0.22, 0.18) if cuts else 1.0
    drawn = jax.random.normal(stream_key, dims, jnp.float32) * width * factor_of
    return jnp.minimum(jnp.maximum(drawn, -most), most).astype(kind)


def bell_draw_with(own_key, dims, width, reach, cuts, heavy, kind=jnp.bfloat16):
    drawn = width * jax.random.normal(own_key, dims, jnp.float32)
    if cuts:
        drawn = drawn * shard_levels(own_key, dims, cuts, -0.22, 0.18)
    return jnp.clip(with_spikes(drawn, jax.random.fold_in(own_key, 3), *heavy), -reach, reach).astype(kind)


def setup_inputs(seed: int = 0) -> dict:
    key_of = jax.random.split(jax.random.key(seed), 21)
    tokens = bell_draw_with(key_of[0], (TOKENS, D), 1.0, 6.0, ((0, 8),), (0, 1, 8, 2.0))
    out_grad = bell_draw_with(key_of[1], (TOKENS, D), 1.0, 6.0, ((0, 8),), (0, 1, 8, 2.0))
    pair_start = draw_pair_start(jax.random.fold_in(key_of[20], 71), 0)
    caption_len = draw_caption_len(jax.random.fold_in(key_of[20], 71), 0)
    region_len = draw_region_len(jax.random.fold_in(key_of[20], 71), 0)
    w_query = gaussian(key_of[5], (D, D), D ** -0.5, 0.21875, ((1, 4),))
    w_key = gaussian(key_of[6], (D, D), D ** -0.5, 0.21875, ((1, 4),))
    w_value = gaussian(key_of[7], (D, D), D ** -0.5, 0.21875, ((1, 4),))
    b_query = gaussian(key_of[8], (D,), 0.5, 3.0, ((0, 4),), jnp.float32)
    b_value = gaussian(key_of[9], (D,), 0.5, 3.0, ((0, 4),), jnp.float32)
    w_out = gaussian(key_of[10], (D, D), (D // 32) ** -0.5, 1.25, ((0, 4),))
    b_out = gaussian(key_of[11], (D,), 0.3, 2.0, (), jnp.float32)
    mixed_gain = jnp.clip(1.0 + 0.1 * jax.random.normal(key_of[12], (D,), jnp.float32), 0.5, 1.5)
    mixed_shift = gaussian(key_of[13], (D,), 0.3, 2.0, (), jnp.float32)
    w_up = gaussian(key_of[14], (D, FF), D ** -0.5, 0.21875, ((1, 4),))
    b_up = gaussian(key_of[15], (FF,), 0.5, 3.0, ((0, 4),), jnp.float32)
    w_down = gaussian(key_of[16], (FF, D), FF ** -0.5, 0.109375, ((0, 4),))
    b_down = gaussian(key_of[17], (D,), 0.3, 2.0, (), jnp.float32)
    final_gain = jnp.clip(1.0 + 0.1 * jax.random.normal(key_of[18], (D,), jnp.float32), 0.5, 1.5)
    final_shift = gaussian(key_of[19], (D,), 0.3, 2.0, (), jnp.float32)
    return {"tokens": tokens, "out_grad": out_grad, "pair_start": pair_start, "caption_len": caption_len, "region_len": region_len, "w_query": w_query, "w_key": w_key, "w_value": w_value, "b_query": b_query, "b_value": b_value, "w_out": w_out, "b_out": b_out, "mixed_gain": mixed_gain, "mixed_shift": mixed_shift, "w_up": w_up, "b_up": b_up, "w_down": w_down, "b_down": b_down, "final_gain": final_gain, "final_shift": final_shift}


@jax.custom_vjp
def low(v):
    return lax.optimization_barrier(v.astype(jnp.bfloat16)).astype(jnp.float32)

@jax.custom_vjp
def low_back(v):
    return v

def low_keep(v):
    return (low(v), None)

def low_pass(kept, grad):
    return (grad,)

def back_keep(v):
    return (v, None)

def back_low(kept, grad):
    return (low(grad),)
low.defvjp(low_keep, low_pass)
low_back.defvjp(back_keep, back_low)
HIGH = lax.Precision.HIGHEST
epsilon = 1e-05

def pair_ids(pair_start, caption_len, region_len):
    places = jnp.arange(BIN, dtype=jnp.int32)
    finish = pair_start + caption_len + region_len
    inside = (places[None, :, None] >= pair_start[:, None, :]) & (places[None, :, None] < finish[:, None, :])
    numbers = jnp.arange(1, SLOTS + 1, dtype=jnp.int32)
    return lax.optimization_barrier(jnp.max(jnp.where(inside, numbers, 0), axis=2)).astype(jnp.int32)

def layer_norm(value, norm_gain, norm_shift):
    centered = value - lax.optimization_barrier(jnp.mean(value, axis=-1, keepdims=True))
    inverse = lax.rsqrt(lax.optimization_barrier(jnp.mean(centered * centered, axis=-1, keepdims=True)) + epsilon)
    return centered * inverse * norm_gain + norm_shift

def attend_block(items):
    queries, keys, values, labels = items
    scores = jnp.einsum('qhd,khd->hqk', queries, keys, precision=HIGH) * HD ** (-0.5)
    scores = low_back(scores)
    allowed = labels[:, None] == labels[None, :]
    scores = jnp.where(allowed[None], scores, -1e+30)
    weights = jax.nn.softmax(scores, axis=-1)
    return jnp.einsum('hqk,khd->qhd', low(weights), values, precision=HIGH)
attend_checked = jax.checkpoint(attend_block)

def layer(params, inputs, labels):
    w_query, w_key, w_value, b_query, b_value, w_out, b_out, mixed_gain, mixed_shift, w_up, b_up, w_down, b_down, final_gain, final_shift = params
    count = inputs.shape[0]
    groups = N_MP
    group_heads = HEADS // groups
    group_units = FF // groups
    copies = low_back(jnp.broadcast_to(inputs[:, None, :], (count, groups, D)))

    def project(weight):
        return jnp.einsum('ngd,dghk->nghk', copies, weight.reshape(D, groups, group_heads, HD), precision=HIGH)
    queries = low(low_back(project(w_query) + b_query.reshape(groups, group_heads, HD)))
    keys = low(low_back(project(w_key)))
    values = low(low_back(project(w_value) + b_value.reshape(groups, group_heads, HD)))
    shaped = (count // BIN, BIN, HEADS, HD)
    mixed = lax.map(attend_checked, (queries.reshape(shaped), keys.reshape(shaped), values.reshape(shaped), labels))
    mixed = low(low_back(mixed.reshape(count, groups, group_heads, HD)))
    parts = low(jnp.einsum('nghk,ghkd->ngd', mixed, w_out.reshape(groups, group_heads, HD, D), precision=HIGH))
    attended = low_back(lax.optimization_barrier(jnp.sum(parts, axis=1)) + b_out)
    normed = layer_norm(inputs + attended, mixed_gain, mixed_shift)
    rounded = low(normed)
    spread_rows = low_back(jnp.broadcast_to(rounded[:, None, :], (count, groups, D)))
    inner = jnp.einsum('ngd,dgf->ngf', spread_rows, w_up.reshape(D, groups, group_units), precision=HIGH)
    inner = low_back(inner + b_up.reshape(groups, group_units))
    hidden = low(jax.nn.gelu(inner, approximate=False))
    parts_down = low(jnp.einsum('ngf,gfd->ngd', hidden, w_down.reshape(groups, group_units, D), precision=HIGH))
    fed = low_back(lax.optimization_barrier(jnp.sum(parts_down, axis=1)) + b_down)
    return layer_norm(normed + fed, final_gain, final_shift)

def reference(tokens, out_grad, pair_start, caption_len, region_len, w_query, w_key, w_value, b_query, b_value, w_out, b_out, mixed_gain, mixed_shift, w_up, b_up, w_down, b_down, final_gain, final_shift):
    params = tuple((item.astype(jnp.float32) for item in (w_query, w_key, w_value, b_query, b_value, w_out, b_out, mixed_gain, mixed_shift, w_up, b_up, w_down, b_down, final_gain, final_shift)))
    group_bins = math.gcd(BINS, max(1, 4096 // BIN))
    span = group_bins * BIN
    rounds = TOKENS // span
    labels_all = pair_ids(pair_start, caption_len, region_len)

    def visit(totals, index):
        start = (index * span).astype(jnp.int32)
        inputs = lax.dynamic_slice_in_dim(tokens, start, span, 0).astype(jnp.float32)
        upstream = lax.dynamic_slice_in_dim(out_grad, start, span, 0).astype(jnp.float32)
        labels = lax.dynamic_slice_in_dim(labels_all, (index * group_bins).astype(jnp.int32), group_bins, 0)
        upstream = upstream * (labels.reshape(span) > 0).astype(jnp.float32)[:, None]

        def forward(weights, rows):
            return layer(weights, rows, labels)
        result, pullback = jax.vjp(forward, params, inputs)
        param_grads, input_grad = pullback(upstream)
        totals = jax.tree.map(jnp.add, totals, param_grads)
        return (totals, (result.astype(jnp.bfloat16), input_grad.astype(jnp.bfloat16)))
    zeros = jax.tree.map(jnp.zeros_like, params)
    totals, (outputs, input_grads) = lax.scan(visit, zeros, jnp.arange(rounds, dtype=jnp.int32))
    layer_out = outputs.reshape(TOKENS, D)
    tokens_grad = input_grads.reshape(TOKENS, D)
    return (layer_out, tokens_grad, totals[0], totals[1], totals[2], totals[3], totals[4], totals[5], totals[6], totals[7], totals[8], totals[9], totals[10], totals[11], totals[12], totals[13], totals[14])
```

```python
import functools

import jax
import jax.numpy as jnp
from jax import lax
from jax.experimental import pallas as pl
from jax.experimental.pallas import tpu as pltpu
from jax.sharding import PartitionSpec as P

HD = 64
BIN = 512
SLOTS = 12
WIDE = 256
CHUNK = 256

EPS = 1e-05
NEG = -1e30
ROOT_HALF = 0.7071067811865476
DENSITY = 0.3989422804014327

F32 = jnp.float32
BF16 = jnp.bfloat16


def mm(a, b):
    return lax.dot_general(a, b, (((1,), (0,)), ((), ())), preferred_element_type=F32)


def mm_nt(a, b):
    return lax.dot_general(a, b, (((1,), (1,)), ((), ())), preferred_element_type=F32)


def mm_tn(a, b):
    return lax.dot_general(a, b, (((0,), (0,)), ((), ())), preferred_element_type=F32)


def shape(dims, dtype):
    return jax.ShapeDtypeStruct(dims, dtype)


def call(body, name, grid, ins, outs, out_shape, args, prefetch=0, scratch=(), aliases=None, flops=0, size=0, trans=0):
    return pl.pallas_call(
        body,
        name=name,
        grid_spec=pltpu.PrefetchScalarGridSpec(
            num_scalar_prefetch=prefetch, grid=grid, in_specs=ins, out_specs=outs, scratch_shapes=list(scratch)
        ),
        out_shape=out_shape,
        input_output_aliases=aliases or {},
        compiler_params=pltpu.CompilerParams(dimension_semantics=("arbitrary",) * len(grid)),
        cost_estimate=pl.CostEstimate(flops=flops, bytes_accessed=size, transcendentals=trans),
    )(*args)


def labels_at(places, block, start_ref, finish_ref):
    found = jnp.zeros_like(places)
    for slot in range(SLOTS):
        inside = (places >= start_ref[block, slot]) & (places < finish_ref[block, slot])
        found = jnp.where(inside, slot + 1, found)
    return found


def attend_forward(meta, starts, finishes, x0, x1, xq, a_ref, bq, bv, *refs):
    q_out, k_out, v_out, e_out, m_out, i_out, a_out = refs[-7:]
    step = pl.program_id(0)
    parity = meta[2]

    @pl.when(step == 0)
    def _():
        lane = lax.broadcasted_iota(jnp.int32, (BIN, WIDE), 1)
        for half, x in enumerate((x0, x1)):
            rows = x[...]
            k_out[0, half] = mm_nt(rows, a_ref[192:448, :]).astype(BF16)
            values = mm_nt(rows, a_ref[384:640, :]) + bv[...]
            v_out[0, half] = jnp.where(lane < 192, values, 1.0).astype(BF16)
        a_out[0] = a_ref[...]

    place = step + parity
    block = place // 2
    queries = (mm_nt(xq[...], a_ref[0:256, :]) + bq[...]).astype(BF16) * jnp.asarray(HD**-0.5, BF16)
    low_lane = lax.broadcasted_iota(jnp.int32, (CHUNK, 128), 1) < HD
    q0, q1 = queries[:, :128], queries[:, 128:]
    zero = jnp.zeros_like(q0)
    masked = (jnp.where(low_lane, q0, zero), jnp.where(low_lane, zero, q0), jnp.where(low_lane, q1, zero))
    for head in range(3):
        q_out[0, head] = masked[head]
    rows_at = lax.broadcasted_iota(jnp.int32, (CHUNK, 1), 0) + CHUNK * lax.rem(place, 2)
    cols_at = lax.broadcasted_iota(jnp.int32, (1, BIN), 1)
    here = meta[0] + block
    allowed = labels_at(rows_at, here, starts, finishes) == labels_at(cols_at, here, starts, finishes)
    v0 = v_out[0, block, :, 0:128]
    low_wide = lax.broadcasted_iota(jnp.int32, (BIN, 128), 1) < HD
    one = jnp.ones_like(v0)
    padded = (jnp.where(low_wide, v0, one), jnp.where(low_wide, one, v0), v_out[0, block, :, 128:256])
    sums = []
    for head in range(3):
        tile = slice(0, 128) if head < 2 else slice(128, 256)
        scores = mm_nt(masked[head], k_out[0, block, :, tile])
        scores = jnp.where(allowed, scores, NEG)
        highest = jnp.max(scores, axis=1, keepdims=True)
        expo = jnp.exp(scores - highest).astype(BF16)
        e_out[0, head] = expo
        sums.append(mm(expo, padded[head]))
    whole0 = jnp.where(low_lane, sums[0], sums[1])
    total0 = pltpu.roll(jnp.where(low_lane, sums[1], sums[0]), HD, 1)
    inv0 = 1.0 / total0
    total1 = pltpu.roll(sums[2], HD, 1)
    inv1 = jnp.where(low_lane, 1.0 / total1, 0.0)
    m_out[0, :, 0:128] = (whole0 * inv0).astype(BF16)
    m_out[0, :, 128:256] = (sums[2] * inv1).astype(BF16)
    i_out[0, :, 0:128] = inv0
    i_out[0, :, 128:256] = inv1


def forward_attention(group, meta, starts, finishes, tokens, weight, bq, bv, before):
    keep = lambda *block: pl.BlockSpec(block, lambda i, *_: (0,) * len(block))
    rows = 3 * CHUNK
    out_shape = [
        shape((4, 3, rows, 128), BF16),
        shape((4, 2, BIN, WIDE), BF16),
        shape((4, 2, BIN, WIDE), BF16),
        shape((4, 3, rows, BIN), BF16),
        shape((4, rows, WIDE), BF16),
        shape((4, rows, WIDE), F32),
        shape((4, 768, 768), BF16),
    ]
    outs = [
        pl.BlockSpec((1, 3, CHUNK, 128), lambda i, *_: (group, 0, i, 0)),
        pl.BlockSpec((1, 2, BIN, WIDE), lambda i, *_: (group, 0, 0, 0)),
        pl.BlockSpec((1, 2, BIN, WIDE), lambda i, *_: (group, 0, 0, 0)),
        pl.BlockSpec((1, 3, CHUNK, BIN), lambda i, *_: (group, 0, i, 0)),
        pl.BlockSpec((1, CHUNK, WIDE), lambda i, *_: (group, i, 0)),
        pl.BlockSpec((1, CHUNK, WIDE), lambda i, *_: (group, i, 0)),
        pl.BlockSpec((1, 768, 768), lambda i, *_: (group, 0, 0)),
    ]
    ins = [
        pl.BlockSpec((BIN, 768), lambda i, meta, *_: (meta[0], 0)),
        pl.BlockSpec((BIN, 768), lambda i, meta, *_: (meta[0] + 1, 0)),
        pl.BlockSpec((CHUNK, 768), lambda i, meta, *_: (meta[1] + i, 0)),
        keep(768, 768),
        keep(1, WIDE),
        keep(1, WIDE),
    ]
    args = [meta, starts, finishes, tokens, tokens, tokens, weight, bq, bv]
    aliases = {}
    if before is not None:
        for position, array in enumerate(before):
            aliases[len(args)] = position
            args.append(array)
            ins.append(pl.BlockSpec(memory_space=pl.ANY))
    return call(
        attend_forward,
        "attend_forward",
        (3,),
        ins,
        outs,
        out_shape,
        args,
        prefetch=3,
        aliases=aliases,
        flops=3_500_000_000,
        size=9_000_000,
        trans=1_200_000,
    )


def project_norm(meta, m_ref, a_ref, x_ref, b_out, gain, shift, normal_out, inverse_out, low_out, lowt_out):
    total = x_ref[...].astype(F32) + b_out[...]
    for group in range(4):
        total += mm(m_ref[group, :, 0:192], a_ref[group])
    centered = total - jnp.mean(total, axis=-1, keepdims=True)
    inverse = lax.rsqrt(jnp.mean(centered * centered, axis=-1, keepdims=True) + EPS)
    normal = centered * inverse
    normal_out[...] = normal
    inverse_out[...] = jnp.broadcast_to(inverse, (CHUNK, 128))
    normed = normal * gain[...] + shift[...]
    low_out[...] = normed.astype(BF16)
    lowt_out[...] = normed.T.astype(BF16)


def project_and_norm(meta, mixed, weights, tokens, b_out, gain, shift):
    rows = 3 * CHUNK
    vector = pl.BlockSpec((1, 768), lambda i, *_: (0, 0))
    return call(
        project_norm,
        "project_norm",
        (3,),
        [
            pl.BlockSpec((4, CHUNK, WIDE), lambda i, *_: (0, i, 0)),
            pl.BlockSpec((4, 192, 768), lambda i, *_: (0, 3, 0)),
            pl.BlockSpec((CHUNK, 768), lambda i, meta, *_: (meta[1] + i, 0)),
            vector,
            vector,
            vector,
        ],
        [
            pl.BlockSpec((CHUNK, 768), lambda i, *_: (i, 0)),
            pl.BlockSpec((CHUNK, 128), lambda i, *_: (i, 0)),
            pl.BlockSpec((CHUNK, 768), lambda i, *_: (i, 0)),
            pl.BlockSpec((768, CHUNK), lambda i, *_: (0, i)),
        ],
        [shape((rows, 768), F32), shape((rows, 128), F32), shape((rows, 768), BF16), shape((768, rows), BF16)],
        [meta, mixed, weights, tokens, b_out, gain, shift],
        prefetch=1,
        flops=906_000_000,
        size=9_000_000,
    )


def feed_forward(x_ref, ua, ub, na, nb, ba, bb, *refs):
    hidden_out, slope_out, u_out, n_out, fed_out = refs[-5:]
    fed_in = refs[0]
    which, step = pl.program_id(0), pl.program_id(1)
    up = jnp.where(which == 0, ua[...], ub[...])
    down = jnp.where(which == 0, na[...], nb[...])
    bias = jnp.where(which == 0, ba[...], bb[...])
    u_out[0] = up
    n_out[0] = down

    @pl.when((which == 0) & (step == 0))
    def _():
        if len(refs) > 5:
            fed_out[...] = fed_in[...]
        else:
            fed_out[...] = jnp.zeros_like(fed_out)

    for part in range(3):
        rows = slice(part * CHUNK, (part + 1) * CHUNK)
        inner = mm(x_ref[rows, :], up) + bias
        half = 0.5 + 0.5 * lax.erf(inner * ROOT_HALF)
        hidden = (inner * half).astype(BF16)
        hidden_out[0, rows, :] = hidden
        slope_out[0, rows, :] = (half + inner * (jnp.exp(-0.5 * inner * inner) * DENSITY)).astype(BF16)
        fed_out[rows, :] += mm(hidden, down)


def forward_feed(side, low, ua, ub, na, nb, ba, bb, fed, before):
    rows = 3 * CHUNK
    first = lambda j, i: jnp.where(j == 0, i, 2)
    second = lambda j, i: jnp.where(j == 0, 0, i)
    ins = [
        pl.BlockSpec((rows, 768), lambda j, i: (0, 0)),
        pl.BlockSpec((768, CHUNK), lambda j, i: (0, first(j, i))),
        pl.BlockSpec((768, CHUNK), lambda j, i: (0, second(j, i))),
        pl.BlockSpec((CHUNK, 768), lambda j, i: (first(j, i), 0)),
        pl.BlockSpec((CHUNK, 768), lambda j, i: (second(j, i), 0)),
        pl.BlockSpec((1, CHUNK), lambda j, i: (0, first(j, i))),
        pl.BlockSpec((1, CHUNK), lambda j, i: (0, second(j, i))),
    ]
    args = [low, ua, ub, na, nb, ba, bb]
    aliases = {}
    if fed is not None:
        ins.append(pl.BlockSpec((rows, 768), lambda j, i: (0, 0)))
        args.append(fed)
        for position, array in enumerate(before):
            aliases[len(args)] = position
            args.append(array)
            ins.append(pl.BlockSpec(memory_space=pl.ANY))
    return call(
        feed_forward,
        "feed_forward",
        (2, 3),
        ins,
        [
            pl.BlockSpec((1, rows, CHUNK), lambda j, i: (2 * side + j, 0, i)),
            pl.BlockSpec((1, rows, CHUNK), lambda j, i: (2 * side + j, 0, i)),
            pl.BlockSpec((1, 768, CHUNK), lambda j, i: (2 * side + j, 0, i)),
            pl.BlockSpec((1, CHUNK, 768), lambda j, i: (2 * side + j, i, 0)),
            pl.BlockSpec((rows, 768), lambda j, i: (0, 0)),
        ],
        [
            shape((4, rows, 768), BF16),
            shape((4, rows, 768), BF16),
            shape((4, 768, 768), BF16),
            shape((4, 768, 768), BF16),
            shape((rows, 768), F32),
        ],
        args,
        aliases=aliases,
        flops=3_620_000_000,
        size=20_000_000,
        trans=2_400_000,
    )


def norm_around(meta, starts, finishes, fed, normal1, og, b_down, gain1, shift1, gain2, shift2, out, grad, low, lowt, sums):
    step = pl.program_id(0)
    second = normal1[...] * gain1[...] + shift1[...] + fed[...] + b_down[...]
    centered = second - jnp.mean(second, axis=-1, keepdims=True)
    inverse = lax.rsqrt(jnp.mean(centered * centered, axis=-1, keepdims=True) + EPS)
    normal = centered * inverse
    out[...] = (normal * gain2[...] + shift2[...]).astype(BF16)
    chunk = meta[1] + step
    rows_at = lax.broadcasted_iota(jnp.int32, (CHUNK, 1), 0) + CHUNK * lax.rem(chunk, 2)
    valid = labels_at(rows_at, chunk // 2, starts, finishes) > 0
    upstream = jnp.where(valid, og[...].astype(F32), 0.0)
    scaled = upstream * gain2[...]
    second_grad = inverse * (
        scaled
        - jnp.mean(scaled, axis=-1, keepdims=True)
        - normal * jnp.mean(scaled * normal, axis=-1, keepdims=True)
    )
    grad[...] = second_grad
    rounded = second_grad.astype(BF16)
    low[...] = rounded
    lowt[...] = second_grad.T.astype(BF16)

    @pl.when(step == 0)
    def _():
        sums[...] = jnp.zeros_like(sums)

    sums[0:1, :] += jnp.sum(upstream * normal, axis=0, keepdims=True)
    sums[1:2, :] += jnp.sum(upstream, axis=0, keepdims=True)
    sums[2:3, :] += jnp.sum(rounded.astype(F32), axis=0, keepdims=True)


def second_norm(meta, starts, finishes, fed, normal1, out_grad, b_down, gain1, shift1, gain2, shift2):
    rows = 3 * CHUNK
    vector = pl.BlockSpec((1, 768), lambda i, *_: (0, 0))
    tile = pl.BlockSpec((CHUNK, 768), lambda i, *_: (i, 0))
    return call(
        norm_around,
        "norm_around",
        (3,),
        [tile, tile, pl.BlockSpec((CHUNK, 768), lambda i, meta, *_: (meta[1] + i, 0))] + [vector] * 5,
        [tile, tile, tile, pl.BlockSpec((768, CHUNK), lambda i, *_: (0, i)), pl.BlockSpec((8, 768), lambda i, *_: (0, 0))],
        [
            shape((rows, 768), BF16),
            shape((rows, 768), F32),
            shape((rows, 768), BF16),
            shape((768, rows), BF16),
            shape((8, 768), F32),
        ],
        [meta, starts, finishes, fed, normal1, out_grad, b_down, gain1, shift1, gain2, shift2],
        prefetch=3,
        flops=20_000_000,
        size=12_000_000,
    )


def outer(left, right, out):
    out[0] = mm(left[...], right[0]).astype(BF16)


def outer_grads(odd, left, right):
    return call(
        outer,
        "outer_grads",
        (2, 2),
        [
            pl.BlockSpec((768, 768), lambda j, i: (0, 0)),
            pl.BlockSpec((1, 768, 384), lambda j, i: (2 * j + odd, 0, i)),
        ],
        pl.BlockSpec((1, 768, 384), lambda j, i: (j, 0, i)),
        shape((2, 768, 768), BF16),
        [left, right],
        flops=1_812_000_000,
        size=6_000_000,
    )


def feed_back(grad, slope, u_ref, n_ref, ig_out, ng_out, sums):
    group, step = pl.program_id(0), pl.program_id(1)

    @pl.when((group == 0) & (step == 0))
    def _():
        ng_out[...] = jnp.zeros_like(ng_out)

    total = jnp.zeros((1, CHUNK), F32)
    for part in range(3):
        rows = slice(part * CHUNK, (part + 1) * CHUNK)
        hidden_grad = mm_nt(grad[rows, :], n_ref[0])
        inner = (hidden_grad * slope[0, rows, :].astype(F32)).astype(BF16)
        ig_out[0, rows, :] = inner
        total += jnp.sum(inner.astype(F32), axis=0, keepdims=True)
        ng_out[rows, :] += mm_nt(inner, u_ref[0])
    sums[0] = jnp.broadcast_to(total, (8, CHUNK))


def backward_feed(grad, slope, ups, downs):
    rows = 3 * CHUNK
    return call(
        feed_back,
        "feed_back",
        (4, 3),
        [
            pl.BlockSpec((rows, 768), lambda j, i: (0, 0)),
            pl.BlockSpec((1, rows, CHUNK), lambda j, i: (j, 0, i)),
            pl.BlockSpec((1, 768, CHUNK), lambda j, i: (j, 0, i)),
            pl.BlockSpec((1, CHUNK, 768), lambda j, i: (j, i, 0)),
        ],
        [
            pl.BlockSpec((1, rows, CHUNK), lambda j, i: (j, 0, i)),
            pl.BlockSpec((rows, 768), lambda j, i: (0, 0)),
            pl.BlockSpec((1, 8, CHUNK), lambda j, i: (j, 0, i)),
        ],
        [shape((4, rows, 768), BF16), shape((rows, 768), F32), shape((4, 8, 768), F32)],
        [grad, slope, ups, downs],
        flops=7_240_000_000,
        size=25_000_000,
    )


def norm_back(ng, second, normal, inverse, gain, grad, low, lowt, sums):
    step = pl.program_id(0)
    total = ng[...] + second[...]
    normal1 = normal[...]
    scaled = total * gain[...]
    first = inverse[:, 0:1] * (
        scaled
        - jnp.mean(scaled, axis=-1, keepdims=True)
        - normal1 * jnp.mean(scaled * normal1, axis=-1, keepdims=True)
    )
    grad[...] = first
    rounded = first.astype(BF16)
    low[...] = rounded
    lowt[...] = first.T.astype(BF16)

    @pl.when(step == 0)
    def _():
        sums[...] = jnp.zeros_like(sums)

    sums[0:1, :] += jnp.sum(total * normal1, axis=0, keepdims=True)
    sums[1:2, :] += jnp.sum(total, axis=0, keepdims=True)
    sums[2:3, :] += jnp.sum(rounded.astype(F32), axis=0, keepdims=True)


def first_norm_back(ng, second, normal, inverse, gain):
    rows = 3 * CHUNK
    tile = pl.BlockSpec((CHUNK, 768), lambda i: (i, 0))
    return call(
        norm_back,
        "norm_back",
        (3,),
        [tile, tile, tile, pl.BlockSpec((CHUNK, 128), lambda i: (i, 0)), pl.BlockSpec((1, 768), lambda i: (0, 0))],
        [tile, tile, pl.BlockSpec((768, CHUNK), lambda i: (0, i)), pl.BlockSpec((8, 768), lambda i: (0, 0))],
        [shape((rows, 768), F32), shape((rows, 768), BF16), shape((768, rows), BF16), shape((8, 768), F32)],
        [ng, second, normal, inverse, gain],
        flops=20_000_000,
        size=12_000_000,
    )


def attend_backward(meta, ag, wo, q_ref, k_ref, v_ref, e_ref, m_ref, i_ref, dq_out, dk_own, dv_own, dk_far, dv_far, dk_acc, dv_acc):
    step = pl.program_id(1)
    parity = meta[2]
    block = (step + parity) // 2

    @pl.when(step == 0)
    def _():
        dk_acc[...] = jnp.zeros_like(dk_acc)
        dv_acc[...] = jnp.zeros_like(dv_acc)

    lane = lax.broadcasted_iota(jnp.int32, (CHUNK, 128), 1)
    low_lane = lane < HD
    mixed_grad = mm_nt(ag[...], wo[0]).astype(BF16).astype(F32)
    grad0 = mixed_grad[:, 0:128] * i_ref[0, :, 0:128]
    grad1 = jnp.concatenate([mixed_grad[:, 128:192], jnp.zeros((CHUNK, HD), F32)], axis=1) * i_ref[0, :, 128:256]
    prod0 = grad0 * m_ref[0, :, 0:128].astype(F32)
    prod1 = grad1 * m_ref[0, :, 128:256].astype(F32)
    centre = (
        jnp.sum(jnp.where(low_lane, prod0, 0.0), axis=1, keepdims=True),
        jnp.sum(jnp.where(low_lane, 0.0, prod0), axis=1, keepdims=True),
        jnp.sum(prod1, axis=1, keepdims=True),
    )
    v0 = v_ref[0, block, :, 0:128]
    low_wide = lax.broadcasted_iota(jnp.int32, (BIN, 128), 1) < HD
    one = jnp.ones_like(v0)
    padded = (jnp.where(low_wide, v0, one), jnp.where(low_wide, one, v0), v_ref[0, block, :, 128:256])
    dq = []
    for head in range(3):
        tile = slice(0, 128) if head < 2 else slice(128, 256)
        own = low_lane if head != 1 else ~low_lane
        base = HD if head != 1 else 0
        part = grad0 if head < 2 else grad1
        high = (-centre[head]).astype(BF16).astype(F32)
        rest = -centre[head] - high
        plain = jnp.where(own, part, 0.0)
        joined = jnp.where(lane == base, high, jnp.where(lane == base + 1, rest, plain)).astype(BF16)
        expo = e_ref[0, head]
        spread = mm_nt(joined, padded[head])
        score_grad = (expo.astype(F32) * spread).astype(BF16)
        dq.append(mm(score_grad, k_ref[0, block, :, tile]))
        dk_acc[block, :, tile] += mm_tn(score_grad, q_ref[0, head])
        dv_acc[block, :, tile] += mm_tn(expo, plain.astype(BF16))
    scale = HD**-0.5
    dq_out[0, :, 0:128] = (jnp.where(low_lane, dq[0], dq[1]) * scale).astype(BF16)
    dq_out[0, :, 128:256] = (dq[2] * scale).astype(BF16)

    @pl.when(step == 2)
    def _():
        for acc, own, far in ((dk_acc, dk_own, dk_far), (dv_acc, dv_own, dv_far)):
            for part in range(3):
                at = part + parity
                own[0, part * CHUNK : (part + 1) * CHUNK, :] = acc[
                    at // 2, pl.ds(pl.multiple_of(CHUNK * lax.rem(at, 2), CHUNK), CHUNK), :
                ].astype(BF16)
            at = 3 * (1 - parity)
            far[0] = acc[at // 2, pl.ds(pl.multiple_of(CHUNK * lax.rem(at, 2), CHUNK), CHUNK), :].astype(BF16)


def backward_attention(meta, attended_grad, weights, queries, keys, values, expo, mixed, inverses):
    rows = 3 * CHUNK
    return call(
        attend_backward,
        "attend_backward",
        (4, 3),
        [
            pl.BlockSpec((CHUNK, 768), lambda r, i, *_: (i, 0)),
            pl.BlockSpec((1, 192, 768), lambda r, i, *_: (r, 3, 0)),
            pl.BlockSpec((1, 3, CHUNK, 128), lambda r, i, *_: (r, 0, i, 0)),
            pl.BlockSpec((1, 2, BIN, WIDE), lambda r, i, *_: (r, 0, 0, 0)),
            pl.BlockSpec((1, 2, BIN, WIDE), lambda r, i, *_: (r, 0, 0, 0)),
            pl.BlockSpec((1, 3, CHUNK, BIN), lambda r, i, *_: (r, 0, i, 0)),
            pl.BlockSpec((1, CHUNK, WIDE), lambda r, i, *_: (r, i, 0)),
            pl.BlockSpec((1, CHUNK, WIDE), lambda r, i, *_: (r, i, 0)),
        ],
        [
            pl.BlockSpec((1, CHUNK, WIDE), lambda r, i, *_: (r, i, 0)),
            pl.BlockSpec((1, rows, WIDE), lambda r, i, *_: (r, 0, 0)),
            pl.BlockSpec((1, rows, WIDE), lambda r, i, *_: (r, 0, 0)),
            pl.BlockSpec((1, CHUNK, WIDE), lambda r, i, *_: (r, 0, 0)),
            pl.BlockSpec((1, CHUNK, WIDE), lambda r, i, *_: (r, 0, 0)),
        ],
        [
            shape((4, rows, WIDE), BF16),
            shape((4, rows, WIDE), BF16),
            shape((4, rows, WIDE), BF16),
            shape((4, CHUNK, WIDE), BF16),
            shape((4, CHUNK, WIDE), BF16),
        ],
        [meta, attended_grad, weights, queries, keys, values, expo, mixed, inverses],
        prefetch=1,
        scratch=[pltpu.VMEM((2, BIN, WIDE), F32), pltpu.VMEM((2, BIN, WIDE), F32)],
        flops=12_000_000_000,
        size=25_000_000,
    )


def project_back(meta, xt, agt, dq, dk, dv, far_k, far_v, mixed, a_ref, base, grads, tg_out, sums, joined):
    step = pl.program_id(0)
    joined[:, 0:192] = dq[0, :, 0:192]
    joined[:, 192:384] = dk[0, :, 0:192]
    joined[:, 384:576] = dv[0, :, 0:192]
    at = pl.ds(pl.multiple_of(2 * CHUNK * (1 - meta[2]), CHUNK), CHUNK)
    joined[at, 192:384] = (joined[at, 192:384].astype(F32) + far_k[0, :, 0:192].astype(F32)).astype(BF16)
    joined[at, 384:576] = (joined[at, 384:576].astype(F32) + far_v[0, :, 0:192].astype(F32)).astype(BF16)
    whole = joined[...]
    grads[0, :, 0:576] = mm(xt[...], whole).astype(BF16)
    grads[0, :, 576:768] = mm(agt[...], mixed[0, :, 0:192]).astype(BF16)
    sums[0, 0:1, :] = jnp.sum(whole.astype(F32), axis=0, keepdims=True)

    @pl.when(step == 0)
    def _():
        tg_out[...] = base[...]

    tg_out[...] += mm(whole, a_ref[0])


def backward_project(odd, meta, xt, agt, dq, dk, dv, far_k, far_v, mixed, weights, base):
    rows = 3 * CHUNK
    full = pl.BlockSpec((768, 768), lambda j, *_: (0, 0))
    per = pl.BlockSpec((1, rows, WIDE), lambda j, *_: (2 * j + odd, 0, 0))
    far = pl.BlockSpec((1, CHUNK, WIDE), lambda j, *_: (2 * j + 1 - odd, 0, 0))
    return call(
        project_back,
        "project_back",
        (2,),
        [
            full,
            full,
            per,
            per,
            per,
            far,
            far,
            per,
            pl.BlockSpec((1, 576, 768), lambda j, *_: (2 * j + odd, 0, 0)),
            full,
        ],
        [pl.BlockSpec((1, 768, 768), lambda j, *_: (j, 0, 0)), full, pl.BlockSpec((1, 8, 576), lambda j, *_: (j, 0, 0))],
        [shape((2, 768, 768), BF16), shape((rows, 768), F32), shape((2, 8, 576), F32)],
        [meta, xt, agt, dq, dk, dv, far_k, far_v, mixed, weights, base],
        prefetch=1,
        scratch=[pltpu.VMEM((rows, 576), BF16)],
        flops=3_200_000_000,
        size=20_000_000,
    )


def swap(array, bit, total):
    return lax.ppermute(array, ("dp", "mp"), [(i, i ^ bit) for i in range(total)])


def pick(array, index, axis):
    return lax.dynamic_index_in_dim(array, index, axis, keepdims=False)


def gather_group(own, total, parity):
    near = swap(own, 1, total)
    rows = own.shape[0] // 2
    part = lax.dynamic_slice_in_dim(own, parity * rows, rows, 0)
    over = swap(part, 2, total)
    other = swap(over, 4, total)
    far = jnp.where(
        parity == 0, jnp.concatenate([over, other], axis=0), jnp.concatenate([other, over], axis=0)
    )
    return own, near, far, swap(far, 1, total)


def halve(array, axis, bit, device_bit, total):
    sent = swap(pick(array, 1 - bit, axis), device_bit, total)
    return (pick(array, bit, axis).astype(F32) + sent.astype(F32)).astype(array.dtype)


def scatter_sum(kept, sent, place, total, n_dp):
    bits = [(place >> k) & 1 for k in range(n_dp.bit_length() - 1)]
    received = swap(sent, 1, total)
    both = (kept.astype(F32) + received.astype(F32)).astype(BF16)
    block = 768 // n_dp
    here = both[0, :, :384].astype(F32) + swap(both[1, :, :384], 2, total).astype(F32)
    here = here.astype(BF16).reshape(n_dp // 2, 2, block, 384)
    here = halve(here, 1, bits[0], 4, total)
    there = both[:, :, 384:].reshape(2, n_dp // 2, 2, block, 384)
    there = halve(there, 2, bits[0], 4, total)
    there = (there[0].astype(F32) + swap(there[1], 2, total).astype(F32)).astype(BF16)
    value = jnp.concatenate([here, there], axis=-1)
    left = n_dp // 2
    for k in range(1, len(bits)):
        value = value.reshape(left // 2, 2, block, 768)
        value = halve(value, 1, bits[k], 4 << k, total)
        left //= 2
    return value.reshape(block, 768)


def scatter_vectors(vectors, place, total, n_dp):
    value = vectors[0::2] + swap(vectors[1::2], 1, total)
    value = value[0] + swap(value[1], 2, total)
    left = n_dp
    for k in range(n_dp.bit_length() - 1):
        value = value.reshape(left // 2, 2, -1)
        value = halve(value, 1, (place >> k) & 1, 4 << k, total)
        left //= 2
    return value.reshape(-1)


def body(
    n_dp,
    tokens,
    out_grad,
    pair_start,
    caption_len,
    region_len,
    w_query,
    w_key,
    w_value,
    b_query,
    b_value,
    w_out,
    b_out,
    mixed_gain,
    mixed_shift,
    w_up,
    b_up,
    w_down,
    b_down,
    final_gain,
    final_shift,
):
    total = 4 * n_dp
    place, member = lax.axis_index("dp"), lax.axis_index("mp")
    parity = place & 1
    core = member & 1
    meta = jnp.stack([3 * (member // 2) + core, 3 * member, core]).astype(jnp.int32)
    finish = pair_start + caption_len + region_len
    row = lambda vector: vector.reshape(1, -1)

    attention_own = jnp.concatenate([w_query.T, w_key.T, w_value.T, w_out], axis=0)
    biases_own = jnp.concatenate([b_query, b_value, b_up])
    attention = gather_group(attention_own, total, parity)
    ups = gather_group(w_up, total, parity)
    downs = gather_group(w_down, total, parity)
    bias_near = swap(biases_own, 1, total)
    bias_far = swap(jnp.stack([biases_own, bias_near]), 2, total)
    biases = (biases_own, bias_near, bias_far[0], bias_far[1])
    wide = lambda vector: jnp.pad(vector, (0, WIDE - vector.shape[0])).reshape(1, WIDE)

    state = None
    for group in range(4):
        bias = biases[group]
        state = forward_attention(
            group, meta, pair_start, finish, tokens, attention[group], wide(bias[:192]), wide(bias[192:384]), state
        )
    queries, keys, values, expo, mixed, inverses, weights = state
    normal1, inverse1, low1, low1_t = project_and_norm(
        meta, mixed, weights, tokens, row(b_out), row(mixed_gain), row(mixed_shift)
    )
    fed, before = None, None
    for side in range(2):
        a, b = 2 * side, 2 * side + 1
        *before, fed = forward_feed(
            side, low1, ups[a], ups[b], downs[a], downs[b], row(biases[a][384:]), row(biases[b][384:]), fed, before
        )
    hidden, slope, up_all, down_all = before
    layer_out, second_grad, fed_grad, fed_grad_t, sums2 = second_norm(
        meta,
        pair_start,
        finish,
        fed,
        normal1,
        out_grad,
        row(b_down),
        row(mixed_gain),
        row(mixed_shift),
        row(final_gain),
        row(final_shift),
    )
    down_sent = outer_grads(1, fed_grad_t, hidden)
    down_kept = outer_grads(0, fed_grad_t, hidden)
    down_sum = scatter_sum(down_kept, down_sent, place, total, n_dp)
    inner_grad, normed_part, up_sums = backward_feed(fed_grad, slope, up_all, down_all)
    up_sent = outer_grads(1, low1_t, inner_grad)
    up_kept = outer_grads(0, low1_t, inner_grad)
    up_sum = scatter_sum(up_kept, up_sent, place, total, n_dp)
    first_grad, attended_grad, attended_grad_t, sums1 = first_norm_back(
        normed_part, second_grad, normal1, inverse1, row(mixed_gain)
    )
    dq, dk, dv, far_k, far_v = backward_attention(
        meta, attended_grad, weights, queries, keys, values, expo, mixed, inverses
    )
    got_k, got_v = swap(far_k, 1, total), swap(far_v, 1, total)
    own_tokens = lax.dynamic_slice_in_dim(tokens, member * 768, 768, 0)
    tokens_t = own_tokens.T
    heads_sent, partial, head_sums_sent = backward_project(
        1, meta, tokens_t, attended_grad_t, dq, dk, dv, got_k, got_v, mixed, weights, first_grad
    )
    heads_kept, whole, head_sums_kept = backward_project(
        0, meta, tokens_t, attended_grad_t, dq, dk, dv, got_k, got_v, mixed, weights, partial
    )
    tokens_grad = whole.astype(BF16)
    heads_sum = scatter_sum(heads_kept, heads_sent, place, total, n_dp)

    head_sums = jnp.stack([head_sums_kept[0, 0], head_sums_sent[0, 0], head_sums_kept[1, 0], head_sums_sent[1, 0]])
    small = 192 // n_dp
    block = 768 // n_dp
    spread = lambda vector: jnp.broadcast_to(vector.reshape(1, n_dp, block), (4, n_dp, block))
    by_member = lambda vector: jnp.stack([pick(vector.reshape(n_dp, 4, small), member ^ r, 1) for r in range(4)])
    vectors = jnp.concatenate(
        [
            head_sums[:, 0:192].reshape(4, n_dp, small),
            head_sums[:, 384:576].reshape(4, n_dp, small),
            up_sums[:, 0].reshape(4, n_dp, block),
            spread(sums1[2]),
            spread(sums2[2]),
            by_member(sums1[0]),
            by_member(sums1[1]),
            by_member(sums2[0]),
            by_member(sums2[1]),
        ],
        axis=2,
    )
    vector = scatter_vectors(vectors, place, total, n_dp)
    cuts, at = [], 0
    for length in (small, small, block, block, block, small, small, small, small):
        cuts.append(vector[at : at + length])
        at += length
    bq_grad, bv_grad, bup_grad, bout_grad, bdown_grad, mg_grad, ms_grad, fg_grad, fs_grad = cuts
    heads_sum = heads_sum.astype(F32)
    return (
        layer_out,
        tokens_grad,
        heads_sum[:, 0:192],
        heads_sum[:, 192:384],
        heads_sum[:, 384:576],
        bq_grad,
        bv_grad,
        heads_sum[:, 576:768].T,
        bout_grad,
        mg_grad,
        ms_grad,
        up_sum.astype(F32),
        bup_grad,
        down_sum.astype(F32).T,
        bdown_grad,
        fg_grad,
        fs_grad,
    )


def solution(mesh):
    n_dp = mesh.shape["dp"]
    placed = (
        P("dp", None),
        P("dp", None),
        P("dp", None),
        P("dp", None),
        P("dp", None),
        P(None, "mp"),
        P(None, "mp"),
        P(None, "mp"),
        P("mp"),
        P("mp"),
        P("mp", None),
        P(),
        P(),
        P(),
        P(None, "mp"),
        P("mp"),
        P("mp", None),
        P(),
        P(),
        P(),
    )
    return jax.shard_map(
        functools.partial(body, n_dp),
        mesh=mesh,
        in_specs=placed,
        out_specs=(
            P(("dp", "mp"), None),
            P(("dp", "mp"), None),
            P("dp", "mp"),
            P("dp", "mp"),
            P("dp", "mp"),
            P(("mp", "dp")),
            P(("mp", "dp")),
            P("mp", "dp"),
            P("dp"),
            P(("dp", "mp")),
            P(("dp", "mp")),
            P("dp", "mp"),
            P(("mp", "dp")),
            P("mp", "dp"),
            P("dp"),
            P(("dp", "mp")),
            P(("dp", "mp")),
        ),
        check_vma=False,
    )
```
